32 devices in a mesh: rep: 4 (over z), shard: 4 (over y, core), ctx: 2 (over x).
Axes of the slice: x: 2, y: 2, z: 4, core: 2. Of those that a mesh axis runs over, the one named last changes fastest.
Arguments:
- tokens: bfloat16 [16, 256, 2048], P(('rep', 'shard'), 'ctx'), may hold values from -6 to 6
- cotangent: bfloat16 [16, 256, 2048], P(('rep', 'shard'), 'ctx'), may hold values from -6 to 6
- seg_ids: int32 [16, 256], P(('rep', 'shard')), may hold values from 0 to 7, never falling along the last dimension, each value on 1 to 128 neighbouring positions
- stretch_order: int32 [16, 2], P(('rep', 'shard')), may hold values from 0 to 1, each once within a row
- attn_norm_gain: bfloat16 [2048], P(('shard', 'ctx')), may hold values from 0.099609375 to 1.8984375
- attn_norm_bias: bfloat16 [2048], P(('shard', 'ctx')), may hold values from -1.5 to 1.5
- w_qkv: bfloat16 [2048, 3072], P(('shard', 'ctx')), may hold values from -0.125 to 0.125
- q_bias: bfloat16 [1024], P(('shard', 'ctx')), may hold values from -20 to 20
- v_bias: bfloat16 [1024], P(('shard', 'ctx')), may hold values from -3 to 3
- w_out: bfloat16 [1024, 2048], P(('shard', 'ctx')), may hold values from -1 to 1
- ffn_norm_gain: bfloat16 [2048], P(('shard', 'ctx')), may hold values from 0.099609375 to 1.8984375
- ffn_norm_bias: bfloat16 [2048], P(('shard', 'ctx')), may hold values from -1.5 to 1.5
- w_gate: bfloat16 [2048, 2816], P(('shard', 'ctx')), may hold values from -0.125 to 0.125
- w_up: bfloat16 [2048, 2816], P(('shard', 'ctx')), may hold values from -0.125 to 0.125
- w_down: bfloat16 [2816, 2048], P(('shard', 'ctx')), may hold values from -0.109375 to 0.109375
Outputs:
- block_out: bfloat16 [16, 256, 2048], P(('rep', 'shard'), 'ctx')
- grad_input: bfloat16 [16, 256, 2048], P(('rep', 'shard'), 'ctx')
- grad_attn_norm_gain: float32 [2048], P(('shard', 'ctx'))
- grad_attn_norm_bias: float32 [2048], P(('shard', 'ctx'))
- grad_qkv: float32 [2048, 3072], P(('shard', 'ctx'))
- grad_q_bias: float32 [1024], P(('shard', 'ctx'))
- grad_v_bias: float32 [1024], P(('shard', 'ctx'))
- grad_out_proj: float32 [1024, 2048], P(('shard', 'ctx'))
- grad_ffn_norm_gain: float32 [2048], P(('shard', 'ctx'))
- grad_ffn_norm_bias: float32 [2048], P(('shard', 'ctx'))
- grad_gate: float32 [2048, 2816], P(('shard', 'ctx'))
- grad_up: float32 [2048, 2816], P(('shard', 'ctx'))
- grad_down: float32 [2816, 2048], P(('shard', 'ctx'))
The draws below stay inside these ranges and needn't reach their ends.
Inputs may be any that keep to these rules, and one draw needn't show every extreme that they name: `seg_ids`: document numbers never fall along a sequence; a document holds at most 128 positions. `stretch_order`: each row names every block of positions once.
All inputs are finite; a program needn't handle non-finite values.
Results may differ from the reference program's by a relative error of at most 0.024.
Values may be sent and summed in bfloat16 or wider, within the bound.
No kernel may reach another device: no remote copies, remote signals or barrier semaphores. Data moves between devices by JAX's collectives and lax.ppermute only.
A program may use at most 384 MiB of HBM per device.

```python
import math
import jax
import jax.numpy as jnp
import numpy as np
from jax import lax

D = 2048
HEADS = 16
HD = 64
FF = 2816
ATTN = 1024
ROT = 16
TOK_DEV = 128
DOCS = 8
SEQ_LEN = 256
SEQS = 16
DOC_MOST = 128
N_CTX = 2


def draw_q_bias(key, part):
    base_key = jax.random.fold_in(jax.random.fold_in(key, 17), 0)
    base = 0.5 * jax.random.normal(base_key, (ATTN,), jnp.float32)
    return jnp.clip(base, -20.0, 20.0).astype(jnp.bfloat16)


def levels(rng, shape, shards, least, largest):
    gain = 1.0
    for position, shards_of in shards:
        draws = jax.random.uniform(jax.random.fold_in(jax.random.fold_in(rng, 6), position), (shards_of,), jnp.float32, least / len(shards), largest / len(shards))
        gain = gain * jnp.repeat(jnp.exp(draws), shape[position] // shards_of).reshape((-1,) + (1,) * (len(shape) - 1 - position))
    return gain


def length_profile(count, total, reach, lean):
    loads = [(1 << 20) // math.isqrt(grade ** lean) + 1 for grade in range(2, count + 1)]
    surplus, given = total - reach - (count - 1), [1] * (count - 1)
    while surplus > 0:
        candidates = [i for i in range(count - 1) if given[i] < reach]
        mass, budget = sum([loads[i] for i in candidates]), surplus
        for i in candidates:
            more = min(reach - given[i], max(1, budget * loads[i] // mass), surplus)
            given[i] = given[i] + more
            surplus = surplus - more
    return np.array([reach] + given)


def ragged_sizes(rng, amount, total, most, slope):
    if amount == 2:
        one = jax.random.randint(rng, (), max(1, total - most), min(most, total - 1) + 1)
        return jnp.stack([one, total - one])
    sizes = jnp.asarray(length_profile(amount, total, most, slope), jnp.int32)
    couples = (amount - 1) // 2
    donor, taker = sizes[1:1 + 2 * couples:2], sizes[2:2 + 2 * couples:2]
    slack = jnp.minimum(donor - 1, most - taker)
    moved = jax.random.randint(jax.random.fold_in(rng, 1), (couples,), 0, 1 << 20) % (slack + 1)
    sizes = sizes.at[1:1 + 2 * couples:2].set(donor - moved).at[2:2 + 2 * couples:2].set(taker + moved)
    return sizes[jax.random.permutation(jax.random.fold_in(rng, 2), amount)]


def scatter_about(key, extent, width, reach, shards=(), held_as=jnp.bfloat16):
    values = width * jax.random.normal(key, extent, jnp.float32)
    if shards:
        values = values * levels(key, extent, shards, -0.22, 0.18)
    return jnp.clip(values, -reach, reach).astype(held_as)


def setup_inputs(seed: int = 0) -> dict:
    seeds = jax.random.split(jax.random.key(seed), 16)
    tokens = scatter_about(seeds[0], (SEQS, SEQ_LEN, D), 1.0, 6.0, ((0, 16), (1, 2)))
    cotangent = scatter_about(seeds[1], (SEQS, SEQ_LEN, D), 1.0, 6.0, ((0, 16), (1, 2)))
    seg_ids = jax.vmap(lambda own: jnp.searchsorted(jnp.cumsum(ragged_sizes(own, DOCS, SEQ_LEN, DOC_MOST, 0)), jnp.arange(SEQ_LEN), side="right"))(jax.random.split(seeds[2], SEQS)).reshape((SEQS, SEQ_LEN)).astype(jnp.int32)
    stretch_order = jax.vmap(lambda own: jax.random.permutation(own, N_CTX))(jax.random.split(seeds[3], SEQS)).reshape((SEQS, N_CTX)).astype(jnp.int32)
    attn_norm_gain = jnp.clip(1.0 + 0.18 * jax.random.normal(seeds[4], (D,), jnp.float32), 0.099609375, 1.8984375).astype(jnp.bfloat16)
    attn_norm_bias = scatter_about(seeds[5], (D,), 0.3, 1.5, ((0, 8),))
    w_qkv = scatter_about(seeds[6], (D, 3 * ATTN), D ** -0.5, 0.125, ((0, 8),))
    q_bias = draw_q_bias(jax.random.fold_in(seeds[15], 71), 0)
    v_bias = scatter_about(seeds[8], (ATTN,), 0.5, 3.0, ((0, 8),))
    w_out = scatter_about(seeds[9], (ATTN, D), (ATTN // 32) ** -0.5, 1.0, ((0, 8),))
    ffn_norm_gain = jnp.clip(1.0 + 0.18 * jax.random.normal(seeds[10], (D,), jnp.float32), 0.099609375, 1.8984375).astype(jnp.bfloat16)
    ffn_norm_bias = scatter_about(seeds[11], (D,), 0.3, 1.5, ((0, 8),))
    w_gate = scatter_about(seeds[12], (D, FF), D ** -0.5, 0.125, ((0, 8),))
    w_up = scatter_about(seeds[13], (D, FF), D ** -0.5, 0.125, ((0, 8),))
    w_down = scatter_about(seeds[14], (FF, D), FF ** -0.5, 0.109375, ((0, 8),))
    return {"tokens": tokens, "cotangent": cotangent, "seg_ids": seg_ids, "stretch_order": stretch_order, "attn_norm_gain": attn_norm_gain, "attn_norm_bias": attn_norm_bias, "w_qkv": w_qkv, "q_bias": q_bias, "v_bias": v_bias, "w_out": w_out, "ffn_norm_gain": ffn_norm_gain, "ffn_norm_bias": ffn_norm_bias, "w_gate": w_gate, "w_up": w_up, "w_down": w_down}


EPSILON = 1e-05
ROPE_BASE = 10000.0
MASKED = -1e+30

def normalize(values, norm_gain, norm_shift):
    center = values - lax.optimization_barrier(jnp.mean(values, axis=-1, keepdims=True))
    scaled = lax.rsqrt(lax.optimization_barrier(jnp.mean(center * center, axis=-1, keepdims=True)) + EPSILON)
    normed = center * scaled
    return (normed * norm_gain.astype(jnp.float32) + norm_shift.astype(jnp.float32), normed, scaled)

def normalize_back(grad_norm, normed, scaled, norm_gain):
    weighted = grad_norm * norm_gain.astype(jnp.float32)
    return scaled * (weighted - lax.optimization_barrier(jnp.mean(weighted, axis=-1, keepdims=True)) - normed * lax.optimization_barrier(jnp.mean(weighted * normed, axis=-1, keepdims=True)))

def rotary_tables(positions):
    half_dims = ROT // 2
    frequencies = jnp.exp(-math.log(ROPE_BASE) * 2.0 * jnp.arange(half_dims, dtype=jnp.float32) / ROT)
    angles = positions.astype(jnp.float32)[:, None] * frequencies[None, :]
    return (jnp.cos(angles), jnp.sin(angles))

def rotate(values, cosine_table, sine_table, inverse):
    half_dims = ROT // 2
    first_half = values[..., :half_dims]
    second_half = values[..., half_dims:ROT]
    cos_part = cosine_table[:, None, :]
    sin_part = sine_table[:, None, :]
    if inverse:
        new_first = first_half * cos_part + second_half * sin_part
        new_second = second_half * cos_part - first_half * sin_part
    else:
        new_first = first_half * cos_part - second_half * sin_part
        new_second = second_half * cos_part + first_half * sin_part
    return jnp.concatenate([new_first, new_second, values[..., ROT:]], axis=-1)

def head_forward(query_head, key_head, value_head, allowed):
    scale_factor = 1.0 / math.sqrt(HD)
    scores = jnp.dot(query_head, key_head.T, preferred_element_type=jnp.float32) * scale_factor
    scores = jnp.where(allowed, scores, MASKED)
    row_top = lax.optimization_barrier(jnp.max(scores, axis=-1, keepdims=True))
    weights = jnp.where(allowed, jnp.exp(scores - row_top), 0.0)
    row_total = lax.optimization_barrier(jnp.sum(weights, axis=-1, keepdims=True))
    mixed = jnp.dot(weights.astype(jnp.bfloat16), value_head, preferred_element_type=jnp.float32) / row_total
    return (mixed, (row_top + jnp.log(row_total))[:, 0])

def head_backward(query_head, key_head, value_head, grad_head, delta_head, lse_head, allowed):
    scale_factor = 1.0 / math.sqrt(HD)
    scores = jnp.dot(query_head, key_head.T, preferred_element_type=jnp.float32) * scale_factor
    probs = jnp.where(allowed, jnp.exp(scores - lse_head[:, None]), 0.0)
    grad_probs = jnp.dot(grad_head, value_head.T, preferred_element_type=jnp.float32)
    grad_scores = (probs * (grad_probs - delta_head[:, None])).astype(jnp.bfloat16)
    grad_value = jnp.dot(probs.astype(jnp.bfloat16).T, grad_head, preferred_element_type=jnp.float32)
    grad_query = jnp.dot(grad_scores, key_head, preferred_element_type=jnp.float32) * scale_factor
    grad_key = jnp.dot(grad_scores.T, query_head, preferred_element_type=jnp.float32) * scale_factor
    return (grad_query, grad_key, grad_value)

def heads_first(array):
    return jnp.transpose(array, (1, 0, 2))

def sequence_pass(totals, inputs, params):
    seq_tokens, seq_cot, seq_seg, seq_order = inputs
    norm1_gain, norm1_bias, qkv_weight, query_bias, value_bias, out_weight, norm2_gain, norm2_bias, gate_weight, up_weight, down_weight = params
    blocks_count = seq_order.shape[0]
    positions = (seq_order[:, None] * TOK_DEV + jnp.arange(TOK_DEV, dtype=jnp.int32)[None, :]).reshape(blocks_count * TOK_DEV)
    doc_ids = jnp.take(seq_seg, positions)
    allowed = (doc_ids[:, None] == doc_ids[None, :]) & (positions[None, :] <= positions[:, None])
    cosine_table, sine_table = rotary_tables(positions)
    row_count = positions.shape[0]
    first_float, normed_one, scaled_one = normalize(seq_tokens.astype(jnp.float32), norm1_gain, norm1_bias)
    first_in = first_float.astype(jnp.bfloat16)
    projected = jnp.dot(first_in, qkv_weight, preferred_element_type=jnp.float32)
    queries = projected[:, :ATTN] + query_bias.astype(jnp.float32)
    keys_pre = projected[:, ATTN:2 * ATTN]
    values = (projected[:, 2 * ATTN:] + value_bias.astype(jnp.float32)).astype(jnp.bfloat16)
    queries = rotate(queries.reshape(row_count, HEADS, HD), cosine_table, sine_table, False).astype(jnp.bfloat16)
    keys_rot = rotate(keys_pre.reshape(row_count, HEADS, HD), cosine_table, sine_table, False).astype(jnp.bfloat16)
    values = values.reshape(row_count, HEADS, HD)
    query_heads = heads_first(queries)
    key_heads = heads_first(keys_rot)
    value_heads = heads_first(values)

    def forward_one(stacked):
        return head_forward(stacked[0], stacked[1], stacked[2], allowed)
    mixed, lse = lax.map(forward_one, (query_heads, key_heads, value_heads))
    attended = heads_first(mixed).reshape(row_count, ATTN).astype(jnp.bfloat16)
    mid_resid = seq_tokens.astype(jnp.float32) + jnp.dot(attended, out_weight, preferred_element_type=jnp.float32)
    second_float, normed_two, scaled_two = normalize(mid_resid, norm2_gain, norm2_bias)
    second_in = second_float.astype(jnp.bfloat16)
    gate_pre = jnp.dot(second_in, gate_weight, preferred_element_type=jnp.float32)
    up_proj = jnp.dot(second_in, up_weight, preferred_element_type=jnp.float32)
    sigmoid_gate = jax.nn.sigmoid(gate_pre)
    hidden = (gate_pre * sigmoid_gate * up_proj).astype(jnp.bfloat16)
    block_out = (mid_resid + jnp.dot(hidden, down_weight, preferred_element_type=jnp.float32)).astype(jnp.bfloat16)
    grad_down = jnp.dot(hidden.T, seq_cot, preferred_element_type=jnp.float32)
    grad_hidden = jnp.dot(seq_cot, down_weight.T, preferred_element_type=jnp.float32)
    grad_gate_pre = (grad_hidden * up_proj * sigmoid_gate * (1.0 + gate_pre * (1.0 - sigmoid_gate))).astype(jnp.bfloat16)
    grad_up_proj = (grad_hidden * gate_pre * sigmoid_gate).astype(jnp.bfloat16)
    grad_gate = jnp.dot(second_in.T, grad_gate_pre, preferred_element_type=jnp.float32)
    grad_up = jnp.dot(second_in.T, grad_up_proj, preferred_element_type=jnp.float32)
    grad_second = jnp.dot(grad_gate_pre, gate_weight.T, preferred_element_type=jnp.float32) + jnp.dot(grad_up_proj, up_weight.T, preferred_element_type=jnp.float32)
    grad_norm2_gain = lax.optimization_barrier(jnp.sum(grad_second * normed_two, axis=0))
    grad_norm2_bias = lax.optimization_barrier(jnp.sum(grad_second, axis=0))
    grad_mid = seq_cot.astype(jnp.float32) + normalize_back(grad_second, normed_two, scaled_two, norm2_gain)
    mid_round = grad_mid.astype(jnp.bfloat16)
    grad_out_proj = jnp.dot(attended.T, mid_round, preferred_element_type=jnp.float32)
    grad_attended = jnp.dot(mid_round, out_weight.T, preferred_element_type=jnp.float32).astype(jnp.bfloat16)
    grad_heads = heads_first(grad_attended.reshape(row_count, HEADS, HD))
    attended_heads = heads_first(attended.reshape(row_count, HEADS, HD))
    delta = lax.optimization_barrier(jnp.sum(grad_heads.astype(jnp.float32) * attended_heads.astype(jnp.float32), axis=-1))

    def backward_one(stacked):
        return head_backward(stacked[0], stacked[1], stacked[2], stacked[3], stacked[4], stacked[5], allowed)
    grad_q_heads, grad_k_heads, grad_v_heads = lax.map(backward_one, (query_heads, key_heads, value_heads, grad_heads, delta, lse))
    grad_queries = rotate(heads_first(grad_q_heads), cosine_table, sine_table, True).reshape(row_count, ATTN)
    grad_keys = rotate(heads_first(grad_k_heads), cosine_table, sine_table, True).reshape(row_count, ATTN)
    grad_values = heads_first(grad_v_heads).reshape(row_count, ATTN)
    qkv_grad = jnp.concatenate([grad_queries, grad_keys, grad_values], axis=1).astype(jnp.bfloat16)
    grad_q_bias = lax.optimization_barrier(jnp.sum(grad_queries, axis=0))
    grad_v_bias = lax.optimization_barrier(jnp.sum(grad_values, axis=0))
    grad_qkv = jnp.dot(first_in.T, qkv_grad, preferred_element_type=jnp.float32)
    grad_first = jnp.dot(qkv_grad, qkv_weight.T, preferred_element_type=jnp.float32)
    grad_norm1_gain = lax.optimization_barrier(jnp.sum(grad_first * normed_one, axis=0))
    grad_norm1_bias = lax.optimization_barrier(jnp.sum(grad_first, axis=0))
    grad_input = (grad_mid + normalize_back(grad_first, normed_one, scaled_one, norm1_gain)).astype(jnp.bfloat16)
    terms = (grad_norm1_gain, grad_norm1_bias, grad_qkv, grad_q_bias, grad_v_bias, grad_out_proj, grad_norm2_gain, grad_norm2_bias, grad_gate, grad_up, grad_down)
    new_totals = tuple((total + term for total, term in zip(totals, terms)))
    return (new_totals, (block_out, grad_input))

def reference(tokens, cotangent, seg_ids, stretch_order, attn_norm_gain, attn_norm_bias, w_qkv, q_bias, v_bias, w_out, ffn_norm_gain, ffn_norm_bias, w_gate, w_up, w_down):
    params = (attn_norm_gain, attn_norm_bias, w_qkv, q_bias, v_bias, w_out, ffn_norm_gain, ffn_norm_bias, w_gate, w_up, w_down)
    zeros_init = tuple((jnp.zeros(param.shape, jnp.float32) for param in params))

    def stepper(totals, inputs):
        return sequence_pass(totals, inputs, params)
    totals, outputs = lax.scan(stepper, zeros_init, (tokens, cotangent, seg_ids, stretch_order))
    block_out, grad_input = outputs
    return (block_out, grad_input, totals[0], totals[1], totals[2], totals[3], totals[4], totals[5], totals[6], totals[7], totals[8], totals[9], totals[10])
```

```python
import math

import jax
import jax.numpy as jnp
from jax import lax
from jax.experimental import pallas as pl
from jax.experimental.pallas import tpu as pltpu
from jax.sharding import PartitionSpec as P

D = 2048
HEADS = 16
HD = 64
FF = 2816
ATTN = 1024
ROT = 16


EPSILON = 1e-05
ROPE_BASE = 10000.0
MASKED = -1e30


def normalize(values, norm_gain, norm_shift):
    center = values - jnp.mean(values, axis=-1, keepdims=True)
    scaled = lax.rsqrt(jnp.mean(center * center, axis=-1, keepdims=True) + EPSILON)
    normed = center * scaled
    return (normed * norm_gain.astype(jnp.float32) + norm_shift.astype(jnp.float32), normed, scaled)


def normalize_back(grad_norm, normed, scaled, norm_gain):
    weighted = grad_norm * norm_gain.astype(jnp.float32)
    return scaled * (
        weighted
        - jnp.mean(weighted, axis=-1, keepdims=True)
        - normed * jnp.mean(weighted * normed, axis=-1, keepdims=True)
    )


def rotary_tables(positions):
    half_dims = ROT // 2
    frequencies = jnp.exp(
        -math.log(ROPE_BASE) * 2.0 * jnp.arange(half_dims, dtype=jnp.float32) / ROT
    )
    angles = positions.astype(jnp.float32)[:, None] * frequencies[None, :]
    return (jnp.cos(angles), jnp.sin(angles))


def rotate(values, cosine_table, sine_table, inverse):
    half_dims = ROT // 2
    first_half = values[..., :half_dims]
    second_half = values[..., half_dims:ROT]
    cos_part = cosine_table[:, None, :]
    sin_part = sine_table[:, None, :]
    if inverse:
        new_first = first_half * cos_part + second_half * sin_part
        new_second = second_half * cos_part - first_half * sin_part
    else:
        new_first = first_half * cos_part - second_half * sin_part
        new_second = second_half * cos_part + first_half * sin_part
    return jnp.concatenate([new_first, new_second, values[..., ROT:]], axis=-1)


def key_places(offset, piece_rows, local_rows, seq_order, seq_seg):
    global_rows = offset + jnp.arange(piece_rows, dtype=jnp.int32)
    source = global_rows // local_rows
    block_ids = jnp.arange(seq_order.shape[0], dtype=jnp.int32)
    stretch_ids = jnp.sum(
        jnp.where(source[:, None] == block_ids[None, :], seq_order[None, :], 0), axis=1
    )
    key_pos = stretch_ids * local_rows + global_rows % local_rows
    return (key_pos, jnp.take(seq_seg, key_pos))


def product_rows(pairs, extra, pick_columns, pick_rows):
    pieces = [
        jnp.dot(pick_columns(left).T, right, preferred_element_type=jnp.float32)
        for left, right in pairs
    ]
    if extra is not None:
        pieces.append(pick_rows(extra))
    if len(pieces) == 1:
        return pieces[0]
    return jnp.concatenate(pieces, axis=1)


def local_gather(
    tokens,
    cotangent,
    seg_ids,
    stretch_order,
    attn_norm_gain,
    attn_norm_bias,
    w_qkv,
    q_bias,
    v_bias,
    w_out,
    ffn_norm_gain,
    ffn_norm_bias,
    w_gate,
    w_up,
    w_down,
):
    seq_tokens = tokens[0]
    seq_cot = cotangent[0]
    seq_seg = seg_ids[0]
    seq_order = stretch_order[0]
    local_rows = seq_tokens.shape[0]
    scale_factor = 1.0 / math.sqrt(HD)
    ctx_index = lax.axis_index("ctx")
    block_ids = jnp.arange(seq_order.shape[0], dtype=jnp.int32)
    own_stretch = jnp.sum(jnp.where(block_ids == ctx_index, seq_order, 0))
    positions = own_stretch * local_rows + jnp.arange(local_rows, dtype=jnp.int32)
    own_docs = jnp.take(seq_seg, positions)
    cosine_table, sine_table = rotary_tables(positions)
    norm1_gain, norm1_bias, qkv_full, norm2_gain, norm2_bias, query_bias, value_bias, out_full = (
        lax.all_gather(attn_norm_gain, ("shard", "ctx"), axis=0, tiled=True),
        lax.all_gather(attn_norm_bias, ("shard", "ctx"), axis=0, tiled=True),
        lax.all_gather(w_qkv, ("shard", "ctx"), axis=0, tiled=True),
        lax.all_gather(ffn_norm_gain, ("shard", "ctx"), axis=0, tiled=True),
        lax.all_gather(ffn_norm_bias, ("shard", "ctx"), axis=0, tiled=True),
        lax.all_gather(q_bias, ("shard", "ctx"), axis=0, tiled=True),
        lax.all_gather(v_bias, ("shard", "ctx"), axis=0, tiled=True),
        lax.all_gather(w_out, ("shard", "ctx"), axis=0, tiled=True),
    )
    first_float, normed_one, scaled_one = normalize(
        seq_tokens.astype(jnp.float32), norm1_gain, norm1_bias
    )
    first_in = first_float.astype(jnp.bfloat16)
    projected = jnp.dot(first_in, qkv_full, preferred_element_type=jnp.float32)
    queries = projected[:, :ATTN] + query_bias.astype(jnp.float32)
    queries = rotate(
        queries.reshape(local_rows, HEADS, HD), cosine_table, sine_table, False
    ).astype(jnp.bfloat16)
    keys_rot = rotate(
        projected[:, ATTN : 2 * ATTN].reshape(local_rows, HEADS, HD),
        cosine_table,
        sine_table,
        False,
    )
    keys_flat = keys_rot.reshape(local_rows, ATTN).astype(jnp.bfloat16)
    values_flat = (projected[:, 2 * ATTN :] + value_bias.astype(jnp.float32)).astype(jnp.bfloat16)
    query_heads = jnp.transpose(queries, (1, 0, 2))
    top_run = jnp.full((HEADS, local_rows), MASKED, jnp.float32)
    key_piece = lax.all_gather(keys_flat, "ctx", axis=0, tiled=True)
    value_piece = lax.all_gather(values_flat, "ctx", axis=0, tiled=True)
    piece_rows = key_piece.shape[0]
    key_pos, key_docs = key_places(jnp.int32(0), piece_rows, local_rows, seq_order, seq_seg)
    allowed = (own_docs[:, None] == key_docs[None, :]) & (key_pos[None, :] <= positions[:, None])
    scores = (
        jnp.einsum(
            "hqd,khd->hqk",
            query_heads,
            key_piece.reshape(piece_rows, HEADS, HD),
            preferred_element_type=jnp.float32,
        )
        * scale_factor
    )
    scores = jnp.where(allowed[None], scores, MASKED)
    new_top = jnp.maximum(top_run, jnp.max(scores, axis=-1))
    weights = jnp.where(allowed[None], jnp.exp(scores - new_top[..., None]), 0.0)
    total_run = jnp.sum(weights, axis=-1)
    accum_run = jnp.einsum(
        "hqk,khd->hqd",
        weights.astype(jnp.bfloat16),
        value_piece.reshape(piece_rows, HEADS, HD),
        preferred_element_type=jnp.float32,
    )
    lse = new_top + jnp.log(total_run)
    mixed = accum_run / total_run[..., None]
    attended = jnp.transpose(mixed, (1, 0, 2)).reshape(local_rows, ATTN).astype(jnp.bfloat16)
    mid_resid = seq_tokens.astype(jnp.float32) + jnp.dot(
        attended, out_full, preferred_element_type=jnp.float32
    )
    gate_full, up_full, down_full = (
        lax.all_gather(w_gate, ("shard", "ctx"), axis=0, tiled=True),
        lax.all_gather(w_up, ("shard", "ctx"), axis=0, tiled=True),
        lax.all_gather(w_down, ("shard", "ctx"), axis=0, tiled=True),
    )
    second_float, normed_two, scaled_two = normalize(mid_resid, norm2_gain, norm2_bias)
    second_in = second_float.astype(jnp.bfloat16)
    gate_pre = jnp.dot(second_in, gate_full, preferred_element_type=jnp.float32)
    up_proj = jnp.dot(second_in, up_full, preferred_element_type=jnp.float32)
    sigmoid_gate = jax.nn.sigmoid(gate_pre)
    hidden = (gate_pre * sigmoid_gate * up_proj).astype(jnp.bfloat16)
    block_out = (mid_resid + jnp.dot(hidden, down_full, preferred_element_type=jnp.float32)).astype(
        jnp.bfloat16
    )
    grad_hidden = jnp.dot(seq_cot, down_full.T, preferred_element_type=jnp.float32)
    grad_gate_pre = (
        grad_hidden * up_proj * sigmoid_gate * (1.0 + gate_pre * (1.0 - sigmoid_gate))
    ).astype(jnp.bfloat16)
    grad_up_proj = (grad_hidden * gate_pre * sigmoid_gate).astype(jnp.bfloat16)
    grad_second = jnp.dot(grad_gate_pre, gate_full.T, preferred_element_type=jnp.float32) + jnp.dot(
        grad_up_proj, up_full.T, preferred_element_type=jnp.float32
    )
    grad_mid = seq_cot.astype(jnp.float32) + normalize_back(
        grad_second, normed_two, scaled_two, norm2_gain
    )
    mid_round = grad_mid.astype(jnp.bfloat16)
    grad_attended = jnp.dot(mid_round, out_full.T, preferred_element_type=jnp.float32).astype(
        jnp.bfloat16
    )
    grad_heads = jnp.transpose(grad_attended.reshape(local_rows, HEADS, HD), (1, 0, 2))
    attended_heads = jnp.transpose(attended.reshape(local_rows, HEADS, HD), (1, 0, 2))
    delta = jnp.sum(grad_heads.astype(jnp.float32) * attended_heads.astype(jnp.float32), axis=-1)
    keys_all, values_all = (
        lax.all_gather(keys_flat, "ctx", axis=0, tiled=True),
        lax.all_gather(values_flat, "ctx", axis=0, tiled=True),
    )
    total_rows = keys_all.shape[0]
    block_rows = math.gcd(total_rows, 512)
    block_count = total_rows // block_rows

    def key_block(grad_query, block_index):
        offset = block_index * block_rows
        key_piece = lax.dynamic_slice_in_dim(keys_all, offset, block_rows, 0).reshape(
            block_rows, HEADS, HD
        )
        value_piece = lax.dynamic_slice_in_dim(values_all, offset, block_rows, 0).reshape(
            block_rows, HEADS, HD
        )
        key_pos, key_docs = key_places(offset, block_rows, local_rows, seq_order, seq_seg)
        allowed = (own_docs[:, None] == key_docs[None, :]) & (
            key_pos[None, :] <= positions[:, None]
        )
        scores = (
            jnp.einsum("hqd,khd->hqk", query_heads, key_piece, preferred_element_type=jnp.float32)
            * scale_factor
        )
        probs = jnp.where(allowed[None], jnp.exp(scores - lse[..., None]), 0.0)
        grad_probs = jnp.einsum(
            "hqd,khd->hqk", grad_heads, value_piece, preferred_element_type=jnp.float32
        )
        grad_scores = (probs * (grad_probs - delta[..., None])).astype(jnp.bfloat16)
        grad_value = jnp.einsum(
            "hqk,hqd->khd",
            probs.astype(jnp.bfloat16),
            grad_heads,
            preferred_element_type=jnp.float32,
        )
        grad_key = (
            jnp.einsum("hqk,hqd->khd", grad_scores, query_heads, preferred_element_type=jnp.float32)
            * scale_factor
        )
        grad_query = (
            grad_query
            + jnp.einsum("hqk,khd->hqd", grad_scores, key_piece, preferred_element_type=jnp.float32)
            * scale_factor
        )
        joined = jnp.concatenate(
            [grad_key.reshape(block_rows, ATTN), grad_value.reshape(block_rows, ATTN)], axis=1
        )
        return (grad_query, joined)

    grad_query_heads, kv_terms = lax.scan(
        key_block,
        jnp.zeros((HEADS, local_rows, HD), jnp.float32),
        jnp.arange(block_count, dtype=jnp.int32),
    )
    kv_grads = lax.psum_scatter(
        kv_terms.reshape(total_rows, 2 * ATTN).astype(jnp.bfloat16),
        "ctx",
        scatter_dimension=0,
        tiled=True,
    ).astype(jnp.float32)
    grad_queries = rotate(
        jnp.transpose(grad_query_heads, (1, 0, 2)), cosine_table, sine_table, True
    ).reshape(local_rows, ATTN)
    grad_keys = rotate(
        kv_grads[:, :ATTN].reshape(local_rows, HEADS, HD), cosine_table, sine_table, True
    ).reshape(local_rows, ATTN)
    grad_values = kv_grads[:, ATTN:]
    qkv_grad = jnp.concatenate([grad_queries, grad_keys, grad_values], axis=1).astype(jnp.bfloat16)
    grad_first = jnp.dot(qkv_grad, qkv_full.T, preferred_element_type=jnp.float32)
    grad_input = (grad_mid + normalize_back(grad_first, normed_one, scaled_one, norm1_gain)).astype(
        jnp.bfloat16
    )
    joined_grad = jnp.concatenate([grad_gate_pre, grad_up_proj], axis=1)
    norm_terms = jnp.stack(
        [
            jnp.sum(grad_first * normed_one, axis=0),
            jnp.sum(grad_first, axis=0),
            jnp.sum(grad_second * normed_two, axis=0),
            jnp.sum(grad_second, axis=0),
        ],
        axis=1,
    )
    bias_terms = jnp.stack([jnp.sum(grad_queries, axis=0), jnp.sum(grad_values, axis=0)], axis=1)
    wide_pairs = ((first_in, qkv_grad), (second_in, joined_grad))
    attn_pairs = ((attended, mid_round),)
    down_pairs = ((hidden, seq_cot),)

    def slicer():
        return (lambda array: array, lambda array: array)

    pick_columns, pick_rows = slicer()
    wide_grads = lax.psum_scatter(
        product_rows(wide_pairs, norm_terms, pick_columns, pick_rows).astype(jnp.bfloat16),
        ("shard", "ctx"),
        scatter_dimension=0,
        tiled=True,
    )
    pick_columns, pick_rows = slicer()
    attn_grads = lax.psum_scatter(
        product_rows(attn_pairs, bias_terms, pick_columns, pick_rows).astype(jnp.bfloat16),
        ("shard", "ctx"),
        scatter_dimension=0,
        tiled=True,
    )
    pick_columns, pick_rows = slicer()
    projection_grads = lax.psum_scatter(
        product_rows(down_pairs, None, pick_columns, pick_rows).astype(jnp.bfloat16),
        ("shard", "ctx"),
        scatter_dimension=0,
        tiled=True,
    )
    wide_total, attn_total, projection_total = (
        lax.psum(wide_grads, "rep").astype(jnp.float32),
        lax.psum(attn_grads, "rep").astype(jnp.float32),
        lax.psum(projection_grads, "rep").astype(jnp.float32),
    )
    norm_base = 3 * ATTN + 2 * FF
    return (
        block_out[None],
        grad_input[None],
        wide_total[:, norm_base],
        wide_total[:, norm_base + 1],
        wide_total[:, : 3 * ATTN],
        attn_total[:, D],
        attn_total[:, D + 1],
        attn_total[:, :D],
        wide_total[:, norm_base + 2],
        wide_total[:, norm_base + 3],
        wide_total[:, 3 * ATTN : 3 * ATTN + FF],
        wide_total[:, 3 * ATTN + FF : norm_base],
        projection_total,
    )


XB, CB, YB = 1, 2, 4
CHIPS = (0, XB, YB, XB | YB)
PLANE = ("shard", "ctx")


def exchangeable(mesh):
    shape = mesh.shape
    return shape["shard"] * shape["ctx"] == 8 and shape["ctx"] == 2 and shape["rep"] == 4


def swap(value, bits):
    return lax.ppermute(value, PLANE, [(i, i ^ bits) for i in range(8)])


def gather_chips(value):
    half = value.shape[1] // 2
    from_x, from_y = swap(value, XB), swap(value, YB)
    low, high = swap(from_x[:, :half], YB), swap(from_y[:, half:], XB)
    return [value, from_x, from_y, jnp.concatenate([low, high], axis=1)]


def gather_direct(value):
    return [value] + [swap(value, bits) for bits in CHIPS[1:]]


def scatter_chips(blocks):
    own, to_x, to_y, to_d = blocks
    half = own.shape[1] // 2
    low, high = swap(to_d[:, :half], XB), swap(to_d[:, half:], YB)
    to_y = jnp.concatenate([to_y[:, :half] + low, to_y[:, half:]], axis=1)
    to_x = jnp.concatenate([to_x[:, :half], to_x[:, half:] + high], axis=1)
    return (
        own.astype(jnp.float32)
        + swap(to_x, XB).astype(jnp.float32)
        + swap(to_y, YB).astype(jnp.float32)
    )


def sum_rep(value):
    place = lax.axis_index("rep")
    middle = (place == 1) | (place == 2)
    half_sum = value + lax.ppermute(value, "rep", [(0, 1), (3, 2)])
    total = half_sum + lax.ppermute(half_sum, "rep", [(1, 2), (2, 1)])
    far = lax.ppermute(total, "rep", [(1, 0), (2, 3)])
    return jnp.where(middle, total, far)


def estimate(flops, nbytes):
    return pl.CostEstimate(flops=int(flops), bytes_accessed=int(nbytes), transcendentals=0)


def place_of(step, core):
    return (step >> 1) * YB + core * CB + (step & 1) * XB


def dot_rows_kernel(me, x, same, other, out):
    step = pl.program_id(0)

    @pl.when(step == 0)
    def _():
        out[...] = jnp.zeros_like(out)

    @pl.when(step < 4)
    def _():
        out[...] += jnp.dot(x[...], same[0], preferred_element_type=jnp.float32)

    @pl.when(step >= 4)
    def _():
        out[...] += jnp.dot(x[...], other[0], preferred_element_type=jnp.float32)


def dot_rows(me, x, same, other):
    rows = x.shape[0]
    _, depth, columns = same.shape
    return pl.pallas_call(
        dot_rows_kernel,
        grid_spec=pltpu.PrefetchScalarGridSpec(
            num_scalar_prefetch=1,
            grid=(8,),
            in_specs=[
                pl.BlockSpec((rows, depth), lambda t, me: (0, place_of(t & 3, t >> 2) ^ me[0])),
                pl.BlockSpec((1, depth, columns), lambda t, me: (jnp.minimum(t, 3), 0, 0)),
                pl.BlockSpec((1, depth, columns), lambda t, me: (jnp.maximum(t - 4, 0), 0, 0)),
            ],
            out_specs=pl.BlockSpec((rows, columns), lambda t, me: (0, 0)),
        ),
        out_shape=jax.ShapeDtypeStruct((rows, columns), jnp.float32),
        cost_estimate=estimate(16 * rows * depth * columns, 2 * rows * 8 * depth + 16 * depth * columns),
    )(me, x, same, other)


def dot_back_kernel(me, dy, same, other, out):
    step = pl.program_id(0)
    contract = (((1,), (1,)), ((), ()))

    @pl.when(step < 4)
    def _():
        out[...] = lax.dot_general(
            dy[...], same[0], contract, preferred_element_type=jnp.float32
        ).astype(out.dtype)

    @pl.when(step >= 4)
    def _():
        out[...] = lax.dot_general(
            dy[...], other[0], contract, preferred_element_type=jnp.float32
        ).astype(out.dtype)


def dot_back(me, dy, same, other):
    rows, columns = dy.shape
    depth = same.shape[1]
    return pl.pallas_call(
        dot_back_kernel,
        grid_spec=pltpu.PrefetchScalarGridSpec(
            num_scalar_prefetch=1,
            grid=(8,),
            in_specs=[
                pl.BlockSpec((rows, columns), lambda t, me: (0, 0)),
                pl.BlockSpec((1, depth, columns), lambda t, me: (jnp.minimum(t, 3), 0, 0)),
                pl.BlockSpec((1, depth, columns), lambda t, me: (jnp.maximum(t - 4, 0), 0, 0)),
            ],
            out_specs=pl.BlockSpec((rows, depth), lambda t, me: (0, place_of(t & 3, t >> 2) ^ me[0])),
        ),
        out_shape=jax.ShapeDtypeStruct((rows, 8 * depth), jnp.bfloat16),
        cost_estimate=estimate(16 * rows * depth * columns, 2 * rows * 8 * depth + 16 * depth * columns),
    )(me, dy, same, other)


def grad_rows_kernel(me, x, dy, out):
    out[0] = lax.dot_general(
        x[...], dy[...], (((0,), (0,)), ((), ())), preferred_element_type=jnp.float32
    ).astype(out.dtype)


def grad_rows_add_kernel(me, x, dy, more, out):
    out[0] = (
        lax.dot_general(x[...], dy[...], (((0,), (0,)), ((), ())), preferred_element_type=jnp.float32)
        + more[0].astype(jnp.float32)
    ).astype(out.dtype)


def grad_rows(me, x, dy, core, more=None):
    rows, columns = dy.shape
    depth = x.shape[1] // 8
    piece = pl.BlockSpec((1, depth, columns), lambda t, me: (t, 0, 0))
    return pl.pallas_call(
        grad_rows_kernel if more is None else grad_rows_add_kernel,
        grid_spec=pltpu.PrefetchScalarGridSpec(
            num_scalar_prefetch=1,
            grid=(4,),
            in_specs=[
                pl.BlockSpec((rows, depth), lambda t, me: (0, place_of(t, core) ^ me[0])),
                pl.BlockSpec((rows, columns), lambda t, me: (0, 0)),
            ]
            + ([] if more is None else [piece]),
            out_specs=piece,
        ),
        out_shape=jax.ShapeDtypeStruct((4, depth, columns), jnp.bfloat16),
        cost_estimate=estimate(8 * rows * depth * columns, 2 * rows * 4 * depth + 8 * depth * columns),
    )(*((me, x, dy) if more is None else (me, x, dy, more)))


def turn(values, cosine, sine_low, sine_high):
    half_dims = ROT // 2
    return (
        values * cosine
        + pltpu.roll(values, values.shape[1] - half_dims, 1) * sine_low
        + pltpu.roll(values, half_dims, 1) * sine_high
    )


def allowed_pairs(row_info, column_info):
    return (row_info[:, 1:2] == column_info[0, 1:2, :]) & (
        column_info[0, 0:1, :] <= row_info[:, 0:1]
    )


def head_lanes(head, lanes):
    return (lax.broadcasted_iota(jnp.int32, (1, lanes), 1) // HD) == head


def masked_scores(query, key, allowed):
    scores = lax.dot_general(
        query, key, (((1,), (1,)), ((), ())), preferred_element_type=jnp.float32
    ) * (1.0 / math.sqrt(HD))
    scores = jnp.where(allowed, scores, MASKED)
    top = jnp.max(scores, axis=-1, keepdims=True)
    weights = jnp.where(allowed, jnp.exp(scores - top), 0.0)
    return weights, jnp.sum(weights, axis=-1, keepdims=True)


def attend_kernel(proj, q_bias, v_bias, cosine, sine_low, sine_high, row_info, column_info, qkv, att):
    lanes = cosine.shape[1]
    width = q_bias.shape[1]
    allowed = allowed_pairs(row_info, column_info)
    for part in range(width // lanes):
        at = part * lanes
        piece = pl.ds(at, lanes)
        query = turn(
            proj[:, at : at + lanes] + q_bias[:, piece], cosine[...], sine_low[...], sine_high[...]
        ).astype(jnp.bfloat16)
        key = turn(
            proj[:, width + at : width + at + lanes], cosine[...], sine_low[...], sine_high[...]
        ).astype(jnp.bfloat16)
        value = (proj[:, 2 * width + at : 2 * width + at + lanes] + v_bias[:, piece]).astype(
            jnp.bfloat16
        )
        qkv[:, at : at + lanes] = query
        qkv[:, width + at : width + at + lanes] = key
        qkv[:, 2 * width + at : 2 * width + at + lanes] = value
        mixed = None
        for head in range(lanes // HD):
            mine = head_lanes(head, lanes)
            weights, total = masked_scores(jnp.where(mine, query, 0), key, allowed)
            product = (
                jnp.dot(weights.astype(jnp.bfloat16), value, preferred_element_type=jnp.float32) / total
            )
            mixed = product if mixed is None else jnp.where(mine, product, mixed)
        att[:, at : at + lanes] = mixed.astype(jnp.bfloat16)


def attend(proj, q_bias, v_bias, tables, row_info, column_info, seq_rows):
    rows, width3 = proj.shape
    width = width3 // 3
    lanes = tables[0].shape[1]
    table = pl.BlockSpec((seq_rows, lanes), lambda s: (s, 0))
    bias = pl.BlockSpec((1, width), lambda s: (0, 0))
    return pl.pallas_call(
        attend_kernel,
        grid=(rows // seq_rows,),
        in_specs=[
            pl.BlockSpec((seq_rows, width3), lambda s: (s, 0)),
            bias,
            bias,
            table,
            table,
            table,
            pl.BlockSpec((seq_rows, 2), lambda s: (s, 0)),
            pl.BlockSpec((1, 2, seq_rows), lambda s: (s, 0, 0)),
        ],
        out_specs=[
            pl.BlockSpec((seq_rows, width3), lambda s: (s, 0)),
            pl.BlockSpec((seq_rows, width), lambda s: (s, 0)),
        ],
        out_shape=[
            jax.ShapeDtypeStruct((rows, width3), jnp.bfloat16),
            jax.ShapeDtypeStruct((rows, width), jnp.bfloat16),
        ],
        cost_estimate=estimate(8 * rows * seq_rows * width, 8 * rows * width3),
    )(proj, q_bias, v_bias, *tables, row_info, column_info)


def attend_back_kernel(qkv, att, grad, cosine, sine_low, sine_high, row_info, column_info, out, sums):
    lanes = cosine.shape[1]
    width = att.shape[1]
    scale = 1.0 / math.sqrt(HD)
    allowed = allowed_pairs(row_info, column_info)
    first = (((0,), (0,)), ((), ()))
    last = (((1,), (1,)), ((), ()))
    sums[...] = jnp.zeros_like(sums)
    for part in range(width // lanes):
        at = part * lanes
        query = qkv[:, at : at + lanes]
        key = qkv[:, width + at : width + at + lanes]
        value = qkv[:, 2 * width + at : 2 * width + at + lanes]
        attended = att[:, at : at + lanes].astype(jnp.float32)
        grad_part = grad[:, at : at + lanes]
        grad_query = grad_key = grad_value = 0.0
        for head in range(lanes // HD):
            mine = head_lanes(head, lanes)
            query_mine = jnp.where(mine, query, 0)
            key_mine = jnp.where(mine, key, 0)
            grad_mine = jnp.where(mine, grad_part, 0)
            weights, total = masked_scores(query_mine, key, allowed)
            probs = weights / total
            grad_probs = lax.dot_general(grad_mine, value, last, preferred_element_type=jnp.float32)
            delta = jnp.sum(grad_mine.astype(jnp.float32) * attended, axis=-1, keepdims=True)
            grad_scores = (probs * (grad_probs - delta)).astype(jnp.bfloat16)
            grad_value += lax.dot_general(
                probs.astype(jnp.bfloat16), grad_mine, first, preferred_element_type=jnp.float32
            )
            grad_query += jnp.dot(grad_scores, key_mine, preferred_element_type=jnp.float32)
            grad_key += lax.dot_general(
                grad_scores, query_mine, first, preferred_element_type=jnp.float32
            )
        grad_query = turn(grad_query * scale, cosine[...], -sine_low[...], -sine_high[...])
        grad_key = turn(grad_key * scale, cosine[...], -sine_low[...], -sine_high[...])
        out[:, at : at + lanes] = grad_query.astype(jnp.bfloat16)
        out[:, width + at : width + at + lanes] = grad_key.astype(jnp.bfloat16)
        out[:, 2 * width + at : 2 * width + at + lanes] = grad_value.astype(jnp.bfloat16)
        sums[0, 0:1, at : at + lanes] = jnp.sum(grad_query, axis=0, keepdims=True)
        sums[0, 1:2, at : at + lanes] = jnp.sum(grad_value, axis=0, keepdims=True)


def attend_back(qkv, att, grad, tables, row_info, column_info, seq_rows):
    rows, width3 = qkv.shape
    width = width3 // 3
    lanes = tables[0].shape[1]
    table = pl.BlockSpec((seq_rows, lanes), lambda s: (s, 0))
    heads = pl.BlockSpec((seq_rows, width), lambda s: (s, 0))
    return pl.pallas_call(
        attend_back_kernel,
        grid=(rows // seq_rows,),
        in_specs=[
            pl.BlockSpec((seq_rows, width3), lambda s: (s, 0)),
            heads,
            heads,
            table,
            table,
            table,
            pl.BlockSpec((seq_rows, 2), lambda s: (s, 0)),
            pl.BlockSpec((1, 2, seq_rows), lambda s: (s, 0, 0)),
        ],
        out_specs=[
            pl.BlockSpec((seq_rows, width3), lambda s: (s, 0)),
            pl.BlockSpec((1, 8, width), lambda s: (s, 0, 0)),
        ],
        out_shape=[
            jax.ShapeDtypeStruct((rows, width3), jnp.bfloat16),
            jax.ShapeDtypeStruct((rows // seq_rows, 8, width), jnp.float32),
        ],
        cost_estimate=estimate(20 * rows * seq_rows * width, 8 * rows * width3),
    )(qkv, att, grad, *tables, row_info, column_info)


def turn_tables(positions):
    lanes = 128
    half_dims = ROT // 2
    feature = jnp.arange(lanes, dtype=jnp.int32) % HD
    turned = feature < ROT
    frequencies = jnp.exp(
        -math.log(ROPE_BASE) * 2.0 * (feature % half_dims).astype(jnp.float32) / ROT
    )
    angles = positions.astype(jnp.float32)[:, None] * frequencies[None, :]
    cosine = jnp.where(turned, jnp.cos(angles), 1.0)
    sine = jnp.sin(angles)
    return (
        cosine,
        jnp.where(feature < half_dims, -sine, 0.0),
        jnp.where(turned & (feature >= half_dims), sine, 0.0),
    )


def local_exchange(
    tokens,
    cotangent,
    seg_ids,
    stretch_order,
    attn_norm_gain,
    attn_norm_bias,
    w_qkv,
    q_bias,
    v_bias,
    w_out,
    ffn_norm_gain,
    ffn_norm_bias,
    w_gate,
    w_up,
    w_down,
):
    own_tokens = tokens[0]
    own_cot = cotangent[0]
    rows = own_tokens.shape[0]
    depth = w_qkv.shape[0]
    head_width = q_bias.shape[0]
    hidden_width = w_down.shape[0]
    seq_rows = 2 * rows
    device = lax.axis_index(PLANE).astype(jnp.int32)
    me = device[None]
    core = (device // CB) & 1
    column = device & 1
    bf16 = jnp.bfloat16

    norms = jnp.stack([attn_norm_gain, attn_norm_bias, ffn_norm_gain, ffn_norm_bias])
    norms_same = jnp.stack(gather_direct(norms))
    norms_other = swap(norms_same, CB)
    pieces = jnp.stack(
        [(norms_other if k & CB else norms_same)[(k & 1) + (k >> 2) * 2] for k in range(8)]
    )
    norms_all = jnp.take(pieces, jnp.arange(8, dtype=jnp.int32) ^ device, axis=0)
    norms_all = jnp.transpose(norms_all, (1, 0, 2)).reshape(4, 8 * depth)
    norm1_gain, norm1_bias, norm2_gain, norm2_bias = norms_all
    biases = jnp.stack([q_bias, v_bias])
    biases_other = swap(biases, CB)
    chip_biases = jnp.where(
        core == 0,
        jnp.concatenate([biases, biases_other], axis=1),
        jnp.concatenate([biases_other, biases], axis=1),
    ).astype(jnp.float32)

    meta = jnp.concatenate([seg_ids[0], stretch_order[0]])
    meta_y = swap(meta, YB)
    positions, docs = [], []
    for one in (meta, meta_y):
        segments, order = one[: seg_ids.shape[1]], one[seg_ids.shape[1] :]
        for place in (column, 1 - column):
            start = lax.dynamic_index_in_dim(order, place, keepdims=False) * rows
            positions.append(start + jnp.arange(rows, dtype=jnp.int32))
            docs.append(lax.dynamic_slice_in_dim(segments, start, rows))
    positions, docs = jnp.concatenate(positions), jnp.concatenate(docs)
    row_info = jnp.stack([positions, docs], axis=1)
    column_info = jnp.stack([positions.reshape(2, seq_rows), docs.reshape(2, seq_rows)], axis=1)
    tables = turn_tables(positions)

    def heads_of(array, owner):
        return lax.dynamic_slice_in_dim(array, owner * head_width, head_width, 1)

    def hidden_of(array, owner):
        return lax.dynamic_slice_in_dim(array, owner * hidden_width, hidden_width, 1)

    def qkv_for(bits):
        owners = [(device ^ bits) & ~CB, (device ^ bits) | CB]
        parts = [w_qkv[:, ATTN * n : ATTN * (n + 1)] for n in range(3)]
        return jnp.concatenate([heads_of(p, o) for p in parts for o in owners], axis=1)

    def gate_up_for(bits):
        owners = [(device ^ bits) & ~CB, (device ^ bits) | CB]
        return jnp.concatenate([hidden_of(p, o) for p in (w_gate, w_up) for o in owners], axis=1)

    tok = jnp.concatenate(gather_chips(own_tokens))
    qkv_same = jnp.stack([qkv_for(0)] + [swap(qkv_for(bits), bits) for bits in CHIPS[1:]])
    qkv_other = swap(qkv_same, CB)
    out_same = jnp.concatenate(gather_direct(w_out))
    out_other = swap(out_same, CB)
    gu_same = jnp.stack([gate_up_for(0)] + [swap(gate_up_for(bits), bits) for bits in CHIPS[1:]])
    gu_other = swap(gu_same, CB)
    down_other = swap(w_down, CB)
    cot = jnp.concatenate(gather_chips(own_cot))

    first_float, normed_one, scaled_one = normalize(tok.astype(jnp.float32), norm1_gain, norm1_bias)
    first_in = first_float.astype(bf16)
    normed_one, scaled_one = normed_one[:rows], scaled_one[:rows]
    projected = dot_rows(me, first_in, qkv_same, qkv_other)
    qkv, att = attend(
        projected, chip_biases[0:1], chip_biases[1:2], tables, row_info, column_info, seq_rows
    )
    att_chips = gather_direct(att)
    ordered = []
    for r, piece in enumerate(att_chips):
        ordered.append(jnp.concatenate([piece[(b ^ r) * rows : ((b ^ r) + 1) * rows] for b in range(4)]))
    low = jnp.concatenate([piece[:, :head_width] for piece in ordered], axis=1)
    high = jnp.concatenate([piece[:, head_width:] for piece in ordered], axis=1)
    att_same, att_other = jnp.where(core == 0, low, high), jnp.where(core == 0, high, low)
    mid_resid = (
        tok.astype(jnp.float32)
        + jnp.dot(att_same, out_same, preferred_element_type=jnp.float32)
        + jnp.dot(att_other, out_other, preferred_element_type=jnp.float32)
    )
    second_float, normed_two, scaled_two = normalize(mid_resid, norm2_gain, norm2_bias)
    second_in = second_float.astype(bf16)
    normed_two, scaled_two = normed_two[:rows], scaled_two[:rows]
    gate_up = dot_rows(me, second_in, gu_same, gu_other)
    chip_hidden = 2 * hidden_width
    gate_pre, up_proj = gate_up[:, :chip_hidden], gate_up[:, chip_hidden:]
    sigmoid_gate = jax.nn.sigmoid(gate_pre)
    hidden = (gate_pre * sigmoid_gate * up_proj).astype(bf16)

    def by_core(array):
        one, two = array[:, : array.shape[1] // 2], array[:, array.shape[1] // 2 :]
        return jnp.where(core == 0, one, two), jnp.where(core == 0, two, one)

    hidden_same, hidden_other = by_core(hidden)
    grad_hidden_same = jnp.dot(cot, w_down.T, preferred_element_type=jnp.float32)
    grad_hidden_other = jnp.dot(cot, down_other.T, preferred_element_type=jnp.float32)
    grad_hidden = jnp.where(
        core == 0,
        jnp.concatenate([grad_hidden_same, grad_hidden_other], axis=1),
        jnp.concatenate([grad_hidden_other, grad_hidden_same], axis=1),
    )
    grad_gate_pre = (
        grad_hidden * up_proj * sigmoid_gate * (1.0 + gate_pre * (1.0 - sigmoid_gate))
    ).astype(bf16)
    grad_up_proj = (grad_hidden * gate_pre * sigmoid_gate).astype(bf16)
    grad_gate_up = jnp.concatenate([grad_gate_pre, grad_up_proj], axis=1)

    def blocks(array):
        return [array[b * rows : (b + 1) * rows] for b in range(4)]

    grad_second = scatter_chips(blocks(dot_back(me, grad_gate_up, gu_same, gu_other)))
    down = (
        jnp.dot(hidden_same, w_down, preferred_element_type=jnp.float32)
        + jnp.dot(hidden_other, down_other, preferred_element_type=jnp.float32)
    ).astype(bf16)
    block_out = (mid_resid[:rows] + scatter_chips(blocks(down))).astype(bf16)

    grad_mid = own_cot.astype(jnp.float32) + normalize_back(
        grad_second, normed_two, scaled_two, norm2_gain
    )
    mid_round = jnp.concatenate(gather_chips(grad_mid.astype(bf16)))

    def by_rows(array):
        return (jnp.dot(array.T, cot, preferred_element_type=jnp.float32))

    down_term = swap(by_rows(hidden_other).astype(bf16), CB)
    grad_down = (by_rows(hidden_same) + down_term.astype(jnp.float32)).astype(bf16)
    gu_term = swap(grad_rows(me, second_in, grad_gate_up, 1), CB)
    gu_grads = grad_rows(me, second_in, grad_gate_up, 0, gu_term)

    chip_out = jnp.where(
        core == 0,
        jnp.concatenate([out_same[:head_width], out_other[:head_width]]),
        jnp.concatenate([out_other[:head_width], out_same[:head_width]]),
    )
    grad_att = jnp.dot(mid_round, chip_out.T, preferred_element_type=jnp.float32).astype(bf16)
    att_keep, att_give = by_core(att)
    out_term = swap(jnp.dot(att_give.T, mid_round, preferred_element_type=jnp.float32).astype(bf16), CB)
    grad_out = (
        jnp.dot(att_keep.T, mid_round, preferred_element_type=jnp.float32)
        + out_term.astype(jnp.float32)
    ).astype(bf16)
    qkv_grad, bias_sums = attend_back(qkv, att, grad_att, tables, row_info, column_info, seq_rows)
    qkv_term = swap(grad_rows(me, first_in, qkv_grad, 1), CB)
    qkv_grads = grad_rows(me, first_in, qkv_grad, 0, qkv_term)
    grad_first = scatter_chips(blocks(dot_back(me, qkv_grad, qkv_same, qkv_other)))
    grad_input = (grad_mid + normalize_back(grad_first, normed_one, scaled_one, norm1_gain)).astype(
        bf16
    )

    def to_owners(pieces, width):
        arrived = [pieces[0]] + [swap(pieces[r], bits) for r, bits in enumerate(CHIPS) if r]
        chips = jnp.stack(arrived)
        here = (device >> 1 & 2) | (device & 1)
        chips = jnp.take(chips, jnp.arange(4, dtype=jnp.int32) ^ here, axis=0)
        parts = pieces.shape[2] // (2 * width)
        out = []
        for n in range(parts):
            cut = [
                chips[2 * (b >> 2) + (b & 1)][
                    :, (2 * n + (b >> 1 & 1)) * width : (2 * n + (b >> 1 & 1) + 1) * width
                ]
                for b in range(8)
            ]
            out.append(jnp.concatenate(cut, axis=1))
        return out

    grad_gate, grad_up = to_owners(gu_grads, hidden_width)
    grad_qkv = jnp.concatenate(to_owners(qkv_grads, head_width), axis=1)

    terms = jnp.stack(
        [
            jnp.sum(grad_first * normed_one, axis=0),
            jnp.sum(grad_first, axis=0),
            jnp.sum(grad_second * normed_two, axis=0),
            jnp.sum(grad_second, axis=0),
        ]
    ).reshape(4, 8, depth)
    terms = jnp.take(jnp.transpose(terms, (1, 0, 2)), jnp.arange(8, dtype=jnp.int32) ^ device, axis=0)
    terms = terms[0::2] + swap(terms[1::2], XB)
    terms = terms[:2] + swap(terms[2:], YB)
    bias_sums = jnp.sum(bias_sums, axis=0)[:2]
    bias_keep, bias_give = by_core(bias_sums)
    small_keep = jnp.concatenate([terms[0].reshape(-1), bias_keep.reshape(-1)])
    small_give = jnp.concatenate([terms[1].reshape(-1), bias_give.reshape(-1)])
    small = small_keep + swap(small_give, CB)
    small = small + lax.ppermute(small, "rep", [(z, z ^ 1) for z in range(4)])
    small = small + lax.ppermute(small, "rep", [(z, z ^ 2) for z in range(4)])
    norm_sums = small[: 4 * depth].reshape(4, depth)
    bias_sums = small[4 * depth :].reshape(2, head_width)

    grad_down, grad_gate, grad_up, grad_out, grad_qkv = [
        sum_rep(g).astype(jnp.float32) for g in (grad_down, grad_gate, grad_up, grad_out, grad_qkv)
    ]
    return (
        block_out[None],
        grad_input[None],
        norm_sums[0],
        norm_sums[1],
        grad_qkv,
        bias_sums[0],
        bias_sums[1],
        grad_out,
        norm_sums[2],
        norm_sums[3],
        grad_gate,
        grad_up,
        grad_down,
    )


def solution(mesh):
    in_specs = (
        P(("rep", "shard"), "ctx", None),
        P(("rep", "shard"), "ctx", None),
        P(("rep", "shard"), None),
        P(("rep", "shard"), None),
        P(("shard", "ctx")),
        P(("shard", "ctx")),
        P(("shard", "ctx"), None),
        P(("shard", "ctx")),
        P(("shard", "ctx")),
        P(("shard", "ctx"), None),
        P(("shard", "ctx")),
        P(("shard", "ctx")),
        P(("shard", "ctx"), None),
        P(("shard", "ctx"), None),
        P(("shard", "ctx"), None),
    )
    out_specs = (
        P(("rep", "shard"), "ctx", None),
        P(("rep", "shard"), "ctx", None),
        P(("shard", "ctx")),
        P(("shard", "ctx")),
        P(("shard", "ctx"), None),
        P(("shard", "ctx")),
        P(("shard", "ctx")),
        P(("shard", "ctx"), None),
        P(("shard", "ctx")),
        P(("shard", "ctx")),
        P(("shard", "ctx"), None),
        P(("shard", "ctx"), None),
        P(("shard", "ctx"), None),
    )
    local = local_exchange if exchangeable(mesh) else local_gather
    return jax.shard_map(local, mesh=mesh, in_specs=in_specs, out_specs=out_specs, check_vma=False)
```
